32 devices in a mesh: row: 4 (over z), col: 8 (over y, x, core).
Axes of the slice: x: 2, y: 2, z: 4, core: 2. Of those that a mesh axis runs over, the one named last changes fastest.
Arguments:
- front: float32 [8192, 8192], P('row', 'col'), may hold values from -6 to 6
- inverses: float32 [2, 512, 512], replicated, may hold values from -2 to 2, as said below
- block_owner: int32 [64, 64], P('row', 'col'), may hold values from -1 to 31, as said below
- block_slot: int32 [64, 64], P('row', 'col'), may hold values from 0 to 47
- parent_in: float32 [1536, 128, 128], P(('row', 'col')), may hold values from -6 to 6
Outputs:
- updated: float32 [8192, 8192], P('row', 'col')
- panels: float32 [8192, 1024], P(('row', 'col'))
- parent_out: float32 [1536, 128, 128], P(('row', 'col'))
The draws below stay inside these ranges and needn't reach their ends.
Inputs may be any that keep to these rules, and one draw needn't show every extreme that they name: Entries of the pivot block inverses. `block_owner`: -1 exactly for blocks above the diagonal (I < J); on one device's 16 x 8 blocks no device is named more than 4 times, and on some device some device is named exactly 4 times.
All inputs are finite; a program needn't handle non-finite values.
Results may differ from the reference program's by a relative error of at most 0.00014.
Values sent between devices are 32-bit elements; how exact they have to be, the bound alone decides.
A program may use at most 128 MiB of HBM per device.

```python
import jax
import jax.numpy as jnp
from jax import lax

PW = 512
BS = 128
PSLOT = 48
F = 8192
NB = 64
TRB = 16
TCB = 8
NROWS = 4
NCOLS = 8
NDEV = 32
PB = 1536


def draw_inverses(key, part):
    key_diag, key_noise = jax.random.split(jax.random.fold_in(key, 11))
    diagonal = jax.random.uniform(key_diag, (2, PW), jnp.float32, 1.0, 2.0)
    noise = jax.random.normal(key_noise, (2, PW, PW), jnp.float32)
    symmetric = (noise + jnp.transpose(noise, (0, 2, 1))) * (0.6 / (PW * 1.4142135))
    identity = jnp.eye(PW, dtype=jnp.float32)
    return symmetric * (1.0 - identity) + identity * (diagonal[:, :, None] / jnp.sqrt(jnp.float32(PW)))


def draw_block_owner(key, part):
    candidates = jax.random.permutation(jax.random.fold_in(key, 5), NDEV).astype(jnp.int32)
    position = jnp.arange(NDEV, dtype=jnp.int32)
    sort_keys = jnp.where(candidates == 1, -2, jnp.where(candidates == NDEV // 2, -1, position)).astype(jnp.int32)
    offsets = candidates[jnp.argsort(sort_keys, stable=True)].astype(jnp.int32)
    index = jnp.arange(NB, dtype=jnp.int32)
    block_row = index[:, None] + jnp.zeros((NB, NB), jnp.int32)
    block_col = index[None, :] + jnp.zeros((NB, NB), jnp.int32)
    lower = (block_row >= block_col).astype(jnp.int32)
    tiles = lower.reshape(NROWS, TRB, NCOLS, TCB).transpose(0, 2, 1, 3).reshape(NROWS, NCOLS, TRB * TCB)
    ranks = jnp.cumsum(tiles, axis=2) - tiles
    ranks = ranks.reshape(NROWS, NCOLS, TRB, TCB).transpose(0, 2, 1, 3).reshape(NB, NB)
    source = block_row // TRB * NCOLS + block_col // TCB
    target = (source + offsets[ranks % NDEV]) % NDEV
    return jnp.where(lower > 0, target, -1).astype(jnp.int32)


def place_ends(entries, own_key, least, largest):
    longest = entries.shape.index(max(entries.shape))
    spots = []
    for shift in (0, 1):
        where = [jax.random.randint(jax.random.fold_in(own_key, axis), (), 0, length) for axis, length in enumerate(entries.shape)]
        where[longest] = (where[longest] + shift) % entries.shape[longest]
        spots.append(tuple(where))
    return entries.at[spots[0]].set(least).at[spots[1]].set(largest)


def block_levels(own_key, extent, cuts, low, largest):
    level = 1.0
    for dim, shards_of in cuts:
        heights = jax.random.uniform(jax.random.fold_in(jax.random.fold_in(own_key, 6), dim), (shards_of,), jnp.float32, low / len(cuts), largest / len(cuts))
        level = level * jnp.repeat(jnp.exp(heights), extent[dim] // shards_of).reshape((-1,) + (1,) * (len(extent) - 1 - dim))
    return level


def bell_draw(rng, dims, width, bound, shards=(), kind=jnp.bfloat16):
    entries = width * jax.random.normal(rng, dims, jnp.float32)
    if shards:
        entries = entries * block_levels(rng, dims, shards, -0.22, 0.18)
    return jnp.clip(entries, -bound, bound).astype(kind)


def setup_inputs(seed: int = 0) -> dict:
    keys = jax.random.split(jax.random.key(seed), 6)
    return {
        "front": bell_draw(keys[0], (F, F), 1.0, 6.0, ((0, 4), (1, 8)), jnp.float32),
        "inverses": draw_inverses(jax.random.fold_in(keys[5], 71), 0),
        "block_owner": draw_block_owner(jax.random.fold_in(keys[5], 71), 0),
        "block_slot": place_ends(jax.random.randint(keys[3], (NB, NB), 0, PSLOT), jax.random.fold_in(keys[3], 1), 0, PSLOT - 1).astype(jnp.int32),
        "parent_in": bell_draw(keys[4], (PB, BS, BS), 1.0, 6.0, ((0, 32),), jnp.float32),
    }


def matmul(left_side, right_side):
    return jnp.dot(left_side, right_side, preferred_element_type=jnp.float32, precision=lax.Precision.HIGHEST)


def reference(front, inverses, block_owner, block_slot, parent_in):
    factor_one = matmul(front[:, 0:PW], inverses[0])
    partial_value = front - matmul(factor_one, front[0:PW, :])
    factor_two = matmul(partial_value[:, PW:2 * PW], inverses[1])
    updated = partial_value - matmul(factor_two, partial_value[PW:2 * PW, :])
    panels = jnp.concatenate([factor_one, factor_two], axis=1)
    blocks = updated.reshape(NB, BS, NB, BS).transpose(0, 2, 1, 3).reshape(NB * NB, BS, BS)
    owners = block_owner.reshape(NB * NB)
    targets = jnp.where(owners >= 0, owners * PSLOT + block_slot.reshape(NB * NB), PB).astype(jnp.int32)
    added = jnp.zeros(parent_in.shape, parent_in.dtype).at[targets].add(blocks, mode="drop")
    parent_out = parent_in + added
    return updated, panels, parent_out
```

```python
import functools

import jax
import jax.numpy as jnp
from jax import lax
from jax.experimental import pallas as pl
from jax.experimental.pallas import tpu as pltpu
from jax.sharding import PartitionSpec as P

MESH = pl.DeviceIdType.MESH
ANY = pl.BlockSpec(memory_space=pl.ANY)
VMEM = pl.BlockSpec(memory_space=pltpu.VMEM)
HBM = pl.BlockSpec(memory_space=pltpu.MemorySpace.HBM)
SMEM = pl.BlockSpec(memory_space=pltpu.SMEM)


def chip_paths(chips):
    order = [i ^ (i >> 1) for i in range(chips)]
    if sorted(order) != list(range(chips)):
        order = list(range(chips))
    return order, [order[0]] + order[1:][::-1]


def pick(value, pairs, default):
    out = jnp.int32(default)
    for key, result in pairs:
        out = jnp.where(value == key, jnp.int32(result), out)
    return out


STEPS = 8
FINE = 2
LAG = 4


def split3(value, axis):
    high = value.astype(jnp.bfloat16)
    low = (value - high.astype(jnp.float32)).astype(jnp.bfloat16)
    return high, low


def front_kernel(
    nrow, ncol, width, cap, brows, bcols, bits,
    packed, front, inverses,
    acc, panels, arrived, marks,
    cut, lbuf, ubuf, ustack, inv, istack, blocks,
    chain_send, side_send, half_recv, row_send, row_recv,
    table, label_rows, labels, where, load_sem, misc_sem, send, recv, mid_recv, label_send, label_recv, gate,
):
    row = lax.axis_index("row")
    col = lax.axis_index("col")
    n = nrow * ncol
    me = row * ncol + col
    chips = ncol // 2
    chip = col // 2
    core = col % 2
    paths = chip_paths(chips)
    nk, rows_all, kc = lbuf.shape
    cols_all = acc.shape[1]
    edge = blocks.shape[1]
    half = rows_all // 2
    ts = half // STEPS
    us = kc // STEPS
    shift = width // ts
    mid = nk // 2
    nexts = [pick(chip, list(zip(p[:-1], p[1:])), 0) for p in paths]
    places = [pick(chip, [(c, at) for at, c in enumerate(p)], 0) for p in paths]
    total = nk * STEPS
    fine = total * FINE
    ls = ts // FINE
    us = us // FINE

    def tile_rows(h, tile):
        return pl.ds(pl.multiple_of(h * half + tile * ts, ts), ts)

    def l_copy(h, t, send_sem, target):
        tile = (t // FINE % STEPS + shift) % STEPS
        first = pl.multiple_of(h * half + tile * ts + t % FINE * ls, ls)
        at = lbuf.at[t // FINE // STEPS, pl.ds(first, ls), :]
        return pltpu.make_async_remote_copy(
            src_ref=at, dst_ref=at,
            send_sem=send_sem.at[h, t], recv_sem=half_recv.at[h, t],
            device_id=(row, target), device_id_type=MESH,
        )

    def u_copy(src, t):
        s = pl.ds(pl.multiple_of(t * us, us), us)
        return pltpu.make_async_remote_copy(
            src_ref=src.at[s, :], dst_ref=ubuf.at[s, :],
            send_sem=row_send.at[t], recv_sem=row_recv.at[t],
            device_id=(row + 1, col), device_id_type=MESH,
        )

    def load(h, i):
        s = tile_rows(h, (i + shift) % STEPS)
        return pltpu.make_async_copy(front.at[s, :], acc.at[s, :], load_sem.at[h, i])

    def load_inv(p):
        return pltpu.make_async_copy(inverses.at[p], inv, misc_sem.at[0])

    load_rows = pltpu.make_async_copy(
        front.at[pl.ds(0, width), :], ubuf.at[pl.ds(0, width), :], misc_sem.at[1]
    )
    piece = rows_all // ncol

    def panel_store(k):
        return pltpu.make_async_copy(
            lbuf.at[k, pl.ds(pl.multiple_of(col * piece, piece), piece), :],
            panels.at[:, pl.ds(k * kc, kc)], misc_sem.at[2 + k],
        )

    def active(r, c):
        return r * brows + brows - 1 >= c * bcols

    def part(index):
        return pl.ds(index * cap, cap)

    def straight(source, target):
        return pltpu.make_async_remote_copy(
            src_ref=blocks.at[part(target)], dst_ref=arrived.at[part(source)],
            send_sem=send.at[target], recv_sem=recv.at[source],
            device_id=(target // ncol, target % ncol), device_id_type=MESH,
        )

    def hop(to_row, to_col):
        target = to_row * ncol + to_col
        return pltpu.make_async_remote_copy(
            src_ref=blocks.at[part(target)], dst_ref=blocks.at[part(to_row * ncol + col)],
            send_sem=send.at[target], recv_sem=mid_recv.at[to_row * ncol + col],
            device_id=(row, to_col), device_id_type=MESH,
        )

    def landed(to_row, from_col):
        return pltpu.make_async_remote_copy(
            src_ref=blocks.at[part(0)], dst_ref=blocks.at[part(to_row * ncol + from_col)],
            send_sem=send.at[0], recv_sem=mid_recv.at[to_row * ncol + from_col],
            device_id=(row, from_col), device_id_type=MESH,
        )

    def relay(to_row, from_col):
        return pltpu.make_async_remote_copy(
            src_ref=blocks.at[part(to_row * ncol + from_col)],
            dst_ref=arrived.at[part(row * ncol + from_col)],
            send_sem=send.at[to_row * ncol + from_col],
            recv_sem=recv.at[row * ncol + from_col],
            device_id=(to_row, col), device_id_type=MESH,
        )

    def label_copy(source, target):
        return pltpu.make_async_remote_copy(
            src_ref=labels.at[target], dst_ref=marks.at[source],
            send_sem=label_send.at[target], recv_sem=label_recv.at[source],
            device_id=(target // ncol, target % ncol), device_id_type=MESH,
        )

    own_blocks = pltpu.make_async_copy(
        blocks.at[part(me)], arrived.at[part(me)], misc_sem.at[2 + nk]
    )
    own_labels = pltpu.make_async_copy(labels.at[me], marks.at[me], misc_sem.at[3 + nk])

    def local_loads():
        @pl.when(col == 0)
        def _():
            load_inv(0).start()

        def start_load(i, carry):
            for h in range(2):
                load(h, i).start()
            return carry

        lax.fori_loop(0, STEPS, start_load, 0)

        @pl.when(row == 0)
        def _():
            load_rows.start()

    barrier = pltpu.get_barrier_semaphore()

    def greet(d, carry):
        other = (me + d) % n
        pl.semaphore_signal(
            barrier, 1, device_id=(other // ncol, other % ncol), device_id_type=MESH
        )
        return carry

    def make_tables():
        count = brows * bcols
        owner = packed[...] >> bits
        slot = (packed[...] & ((1 << bits) - 1)).astype(jnp.float32)
        hit = owner == lax.broadcasted_iota(jnp.int32, (n, count), 0)
        before = lax.broadcasted_iota(jnp.int32, (count, count), 0) < (
            lax.broadcasted_iota(jnp.int32, (count, count), 1)
        )
        rank = jnp.dot(
            jnp.where(hit, 1.0, 0.0), jnp.where(before, 1.0, 0.0),
            preferred_element_type=jnp.float32,
        )
        position = lax.broadcasted_iota(jnp.int32, (n, count), 1).astype(jnp.float32)
        lane = lax.broadcasted_iota(jnp.int32, (n, 128), 1)
        spots = jnp.zeros((n, 128), jnp.float32)
        names = jnp.full((n, 128), -1.0, jnp.float32)
        for q in range(cap):
            chosen = hit & (rank == q)
            spot = jnp.sum(jnp.where(chosen, position, 0.0), axis=1, keepdims=True)
            name = jnp.sum(jnp.where(chosen, slot + 1.0, 0.0), axis=1, keepdims=True) - 1.0
            spots = jnp.where(lane == q, spot, spots)
            names = jnp.where(lane == q, name, names)
        table[...] = spots.astype(jnp.int32)
        label_rows[...] = names.astype(jnp.int32)

        def spread_label(d, carry):
            labels[d] = jnp.broadcast_to(label_rows[pl.ds(d, 1), :], labels.shape[1:])
            return carry

        lax.fori_loop(0, n, spread_label, 0)

    lax.fori_loop(1, n, greet, 0)
    local_loads()
    make_tables()
    pl.semaphore_wait(barrier, n - 1)
    load_table = pltpu.make_async_copy(table, where, misc_sem.at[4 + nk])
    load_table.start()

    @pl.when(core == 1)
    def _():
        def early(u, carry):
            for h in range(2):
                t = u - LAG * jnp.maximum(places[h] - 1, 0)

                @pl.when((t >= 0) & (t < fine))
                def _(h=h, t=t):
                    l_copy(h, t, chain_send, 0).wait_recv()
                    if chips > 1:
                        @pl.when(places[h] < chips - 1)
                        def _():
                            l_copy(h, t, chain_send, nexts[h] * 2 + 1).start()

                    @pl.when(chip > 0)
                    def _():
                        l_copy(h, t, side_send, chip * 2).start()

            return carry

        lax.fori_loop(0, fine + LAG * max(chips - 2, 0), early, 0)

    def stacked(value):
        high, low = split3(value, 1)
        return jnp.concatenate([high, high, low], axis=1)

    def split_rows(source, target, depth):
        high, low = split3(source, 0)
        target[pl.ds(0, depth), :] = high
        target[pl.ds(depth, depth), :] = low
        target[pl.ds(2 * depth, depth), :] = high

    def update(k, i):
        @pl.when(i == 0)
        def _():
            for q in range(cols_all // edge // 2):
                s = pl.ds(q * 2 * edge, 2 * edge)
                split_rows(
                    ubuf[pl.ds(pl.multiple_of(k * kc, kc), kc), s], ustack.at[:, s], kc
                )

        t = k * STEPS + i
        tile = (i + shift) % STEPS

        @pl.when((core == 0) & (col > 0))
        def _():
            for h in range(2):
                for g in range(FINE):
                    l_copy(h, t * FINE + g, chain_send, 0).wait_recv()

        both = jnp.concatenate([lbuf[k, tile_rows(h, tile), :] for h in range(2)], axis=0)
        a = stacked(both)
        for q in range(cols_all // edge // 2):
            s = pl.ds(q * 2 * edge, 2 * edge)
            out = jnp.dot(a, ustack[:, s], preferred_element_type=jnp.float32)
            for h in range(2):
                at = tile_rows(h, tile)
                acc[at, s] = acc[at, s] - out[h * ts:(h + 1) * ts]

        @pl.when(k == nk - 1)
        def _():
            for h in range(2):
                for u in range(ts // edge):
                    at = pl.ds(pl.multiple_of(h * half + tile * ts + u * edge, edge), edge)
                    first = ((h * STEPS + tile) * (ts // edge) + u) * bcols
                    for q in range(bcols):
                        cut[first + q] = acc[at, pl.ds(q * edge, edge)]

        @pl.when((row == 0) & (k == mid - 1) & (i < width // ts))
        def _():
            at = tile_rows(0, tile)
            ubuf[at, :] = acc[at, :]

    def produce(p, i):
        @pl.when(i == 0)
        def _():
            load_inv(p).wait()
            for q in range(width // 256):
                s = pl.ds(q * 256, 256)
                split_rows(inv[:, s], istack.at[:, s], width)

            @pl.when(p == 0)
            def _():
                load_inv(1).start()

        tile = (i + shift) % STEPS
        from_col = pl.ds(pl.multiple_of(p * width, width), width)
        both = jnp.concatenate([acc[tile_rows(h, tile), from_col] for h in range(2)], axis=0)
        a = stacked(both)
        for q in range(mid):
            out = jnp.dot(
                a, istack[:, pl.ds(q * kc, kc)], preferred_element_type=jnp.float32
            )
            for h in range(2):
                lbuf[p * mid + q, tile_rows(h, tile), :] = out[h * ts:(h + 1) * ts]

    def step(t, carry):
        k = t // STEPS
        i = t % STEPS

        @pl.when(k == 0)
        def _():
            for h in range(2):
                load(h, i).wait()

        @pl.when((row == 0) & (t == 0))
        def _():
            load_rows.wait()

        @pl.when(k > 0)
        def _():
            update(k - 1, i)

        @pl.when((col == 0) & ((k == 0) | (k == mid)))
        def _():
            produce(k // mid, i)

        @pl.when(k < nk)
        def _():
            @pl.when(col == 0)
            def _():
                for g in range(FINE):
                    for h in range(2):
                        l_copy(h, t * FINE + g, side_send, 1).start()

            if nrow > 1:
                for g in range(FINE):
                    @pl.when(row > 0)
                    def _(g=g):
                        u_copy(ubuf, t * FINE + g).wait_recv()

                    @pl.when(row < nrow - 1)
                    def _(g=g):
                        u_copy(ubuf, t * FINE + g).start()

        if nrow > 1:
            @pl.when((t == total) & (row < nrow - 1) & ((row == 0) | (core == 1)))
            def _():
                def sent(u, carry):
                    u_copy(ubuf, u).wait_send()
                    return carry

                lax.fori_loop(0, fine, sent, 0)
                pl.semaphore_signal(
                    gate, 1, device_id=(row, col + 1 - 2 * core), device_id_type=MESH
                )

        return carry

    if nrow > 1:
        @pl.when((row == 0) & (core == 1))
        def _():
            pl.semaphore_wait(gate, 1)

    lax.fori_loop(0, total + STEPS, step, 0)

    for k in range(nk):
        panel_store(k).start()

    load_table.wait()
    order = [(nrow // 2 + i) % nrow for i in range(nrow)]

    @pl.when(active(row, col))
    def _():
        def take(to_row, to_col):
            target = to_row * ncol + to_col
            for q in range(cap):
                spot = jnp.clip(where[target, q], 0, cut.shape[0] - 1)
                blocks[target * cap + q] = cut[spot]

        def give(to_row, to_col):
            target = to_row * ncol + to_col
            direct = active(row, to_col) | (to_row == row)

            @pl.when((target != me) & direct)
            def _():
                straight(me, target).start()

            @pl.when(jnp.logical_not(direct))
            def _():
                hop(to_row, to_col).start()

        def pieces(lift):
            def both(j, carry):
                to_col = (col + j) % ncol
                for o in order:
                    to_row = (row + o) % nrow

                    @pl.when((to_row > row) == lift)
                    def _(to_row=to_row):
                        give(to_row, to_col)

                return carry

            lax.fori_loop(0, ncol, both, 0)

        def fill(j, carry):
            to_col = (col + j) % ncol
            for o in order:
                take((row + o) % nrow, to_col)

                @pl.when(j > 0)
                def _(o=o):
                    to_row = (row + o) % nrow

                    @pl.when(to_row <= row)
                    def _():
                        give(to_row, (to_col + ncol - 1) % ncol)

            return carry

        lax.fori_loop(0, ncol, fill, 0)
        for o in order:
            @pl.when((row + o) % nrow <= row)
            def _(o=o):
                give((row + o) % nrow, (col + ncol - 1) % ncol)

        if nrow > 1:
            @pl.when((core == 0) & (row < nrow - 1))
            def _():
                pl.semaphore_wait(gate, 1)

        pieces(True)

        def label_step(d, carry):
            label_copy(me, (me + d) % n).start()
            return carry

        lax.fori_loop(1, n, label_step, 0)
        own_blocks.start()
        own_labels.start()

    def pass_on(act, lift):
        def body(j, carry):
            from_col = 2 * j % ncol + 2 * j // ncol

            @pl.when(active(row, from_col))
            def _():
                for o in order:
                    to_row = (row + o) % nrow

                    @pl.when((to_row != row) & ((to_row > row) == lift))
                    def _(to_row=to_row):
                        act(to_row, from_col)

            return carry

        @pl.when(jnp.logical_not(active(row, col)))
        def _():
            lax.fori_loop(0, ncol, body, 0)

    def forward(to_row, from_col):
        landed(to_row, from_col).wait_recv()
        relay(to_row, from_col).start()

    pass_on(forward, False)
    if nrow > 1:
        @pl.when((core == 0) & (row < nrow - 1) & jnp.logical_not(active(row, col)))
        def _():
            pl.semaphore_wait(gate, 1)

    pass_on(forward, True)

    def drain_l(t, carry):
        for h in range(2):
            @pl.when((col == 0) | ((core == 1) & (chip > 0)))
            def _(h=h):
                l_copy(h, t, side_send, 0).wait_send()

            if chips > 1:
                @pl.when((core == 1) & (places[h] < chips - 1))
                def _(h=h):
                    l_copy(h, t, chain_send, 0).wait_send()

        if nrow > 1:
            @pl.when((row < nrow - 1) & (row > 0) & (core == 0))
            def _():
                u_copy(ubuf, t).wait_send()

        return carry

    lax.fori_loop(0, fine, drain_l, 0)

    for k in range(nk):
        panel_store(k).wait()

    def arrive(s, carry):
        @pl.when((s != me) & active(s // ncol, s % ncol))
        def _():
            label_copy(s, 0).wait_recv()
            straight(s, 0).wait_recv()

        return carry

    lax.fori_loop(0, n, arrive, 0)

    @pl.when(active(row, col))
    def _():
        def drain(d, carry):
            target = (me + d) % n
            label_copy(me, target).wait_send()
            straight(me, target).wait_send()
            return carry

        lax.fori_loop(1, n, drain, 0)
        own_blocks.wait()
        own_labels.wait()

    for lift in (False, True):
        pass_on(lambda to_row, from_col: relay(to_row, from_col).wait_send(), lift)


def front_update(packed, front, inverses, brows, bcols, bits, cap, edge):
    nrow, ncol = lax.axis_size("row"), lax.axis_size("col")
    n = nrow * ncol
    width = inverses.shape[1]
    rows_all, cols_all = front.shape
    kc = width // 2
    nk = 4
    dma = pltpu.SemaphoreType.DMA
    f32, bf16 = jnp.float32, jnp.bfloat16
    shape = jax.ShapeDtypeStruct
    return pl.pallas_call(
        functools.partial(front_kernel, nrow, ncol, width, cap, brows, bcols, bits),
        out_shape=(
            shape(front.shape, f32),
            shape((rows_all // ncol, 2 * width), f32),
            shape((n * cap, edge, edge), f32),
            shape((n, 8, 128), jnp.int32),
        ),
        in_specs=[VMEM, ANY, ANY],
        out_specs=(VMEM, ANY, ANY, VMEM),
        scratch_shapes=[
            pltpu.VMEM((brows * bcols, edge, edge), f32),
            pltpu.VMEM((nk, rows_all, kc), f32),
            pltpu.VMEM((2 * width, cols_all), f32),
            pltpu.VMEM((3 * kc, cols_all), bf16),
            pltpu.VMEM((width, width), f32),
            pltpu.VMEM((3 * width, width), bf16),
            pltpu.VMEM((n * cap, edge, edge), f32),
            dma((2, nk * STEPS * FINE)), dma((2, nk * STEPS * FINE)),
            dma((2, nk * STEPS * FINE)),
            dma((nk * STEPS * FINE,)), dma((nk * STEPS * FINE,)),
            pltpu.VMEM((n, 128), jnp.int32),
            pltpu.VMEM((n, 128), jnp.int32),
            pltpu.VMEM((n, 8, 128), jnp.int32),
            pltpu.SMEM((n, 128), jnp.int32),
            dma((2, STEPS)), dma((5 + nk,)),
            dma((n,)), dma((n,)), dma((n,)), dma((n,)), dma((n,)),
            pltpu.SemaphoreType.REGULAR,
        ],
        compiler_params=pltpu.CompilerParams(
            has_side_effects=True, collective_id=0, vmem_limit_bytes=(34 << 20) + (n - 32) * (16 << 10)
        ),
        name="front_update",
    )(packed, front, inverses)


def add_kernel(
    ncol, brows, bcols, cap, names, parent, arrived, updated, panels,
    out, updated_out, panels_out, marks, parent_sem, name_sem, out_sem,
):
    n = arrived.shape[0] // cap
    parts = out_sem.shape[0] - 1
    rows = updated.shape[0] // parts

    def each(first, count, body):
        def step(s, carry):
            @pl.when(s // ncol * brows + brows - 1 >= s % ncol * bcols)
            def _():
                body(s)

            return carry

        lax.fori_loop(first, first + count, step, 0)

    def put(i):
        s = pl.ds(i * rows, rows)
        return pltpu.make_async_copy(updated.at[s, :], updated_out.at[s, :], out_sem.at[i])

    put_strip = pltpu.make_async_copy(panels, panels_out, out_sem.at[parts])
    whole = pltpu.make_async_copy(parent, out, parent_sem)
    load_names = pltpu.make_async_copy(names, marks, name_sem)
    load_names.start()
    whole.start()
    for i in range(parts):
        put(i).start()
    put_strip.start()
    load_names.wait()
    whole.wait()

    def add(s):
        for k in range(cap):
            m = marks[s, 0, k]

            @pl.when(m >= 0)
            def _(k=k, m=m):
                out[m] = out[m] + arrived[s * cap + k]

    each(0, n, add)
    for i in range(parts):
        put(i).wait()
    put_strip.wait()


def add_blocks(marks, parent, arrived, updated, panels, brows, bcols, cap):
    n = arrived.shape[0] // cap
    parts = 8
    like = lambda x: jax.ShapeDtypeStruct(x.shape, x.dtype)
    return pl.pallas_call(
        functools.partial(add_kernel, lax.axis_size("col"), brows, bcols, cap),
        out_shape=(like(parent), like(updated), like(panels)),
        in_specs=[ANY, VMEM, VMEM, VMEM, VMEM],
        out_specs=(VMEM, HBM, HBM),
        scratch_shapes=[
            pltpu.SMEM(marks.shape, marks.dtype),
            pltpu.SemaphoreType.DMA,
            pltpu.SemaphoreType.DMA,
            pltpu.SemaphoreType.DMA((parts + 1,)),
        ],
        compiler_params=pltpu.CompilerParams(vmem_limit_bytes=24<<20),
        name="add_blocks",
    )(marks, parent, arrived, updated, panels)


def local(front, inverses, block_owner, block_slot, parent_in):
    devices = lax.axis_size("row") * lax.axis_size("col")
    brows, bcols = block_owner.shape
    edge = parent_in.shape[1]
    count = brows * bcols
    cap = max(1, (count + devices - 1) // devices)
    bits = max(1, (parent_in.shape[0] - 1).bit_length())
    packed = ((block_owner << bits) + block_slot).reshape(1, count)
    updated, panels, arrived, marks = front_update(
        packed, front, inverses, brows, bcols, bits, cap, edge
    )
    parent_out, updated, panels = add_blocks(
        marks, parent_in, arrived, updated, panels, brows, bcols, cap
    )
    return (updated, panels, parent_out)


def solution(mesh):
    in_specs = (
        P("row", "col"),
        P(),
        P("row", "col"),
        P("row", "col"),
        P(("row", "col"), None, None),
    )
    out_specs = (P("row", "col"), P(("row", "col"), None), P(("row", "col"), None, None))
    return jax.shard_map(local, mesh=mesh, in_specs=in_specs, out_specs=out_specs, check_vma=False)
```

```python
import functools

import jax
import jax.numpy as jnp
from jax import lax
from jax.experimental import pallas as pl
from jax.experimental.pallas import tpu as pltpu
from jax.sharding import PartitionSpec as P

MESH = pl.DeviceIdType.MESH
ANY = pl.BlockSpec(memory_space=pl.ANY)
VMEM = pl.BlockSpec(memory_space=pltpu.VMEM)
HBM = pl.BlockSpec(memory_space=pltpu.MemorySpace.HBM)
SMEM = pl.BlockSpec(memory_space=pltpu.SMEM)


def chip_paths(chips):
    order = [i ^ (i >> 1) for i in range(chips)]
    if sorted(order) != list(range(chips)):
        order = list(range(chips))
    return order, [order[0]] + order[1:][::-1]


def pick(value, pairs, default):
    out = jnp.int32(default)
    for key, result in pairs:
        out = jnp.where(value == key, jnp.int32(result), out)
    return out


STEPS = 8
FINE = 2
LAG = 4


def split3(value, axis):
    high = value.astype(jnp.bfloat16)
    low = (value - high.astype(jnp.float32)).astype(jnp.bfloat16)
    return high, low


def front_kernel(
    nrow, ncol, width, cap, brows, bcols, bits,
    packed, front, inverses,
    acc, panels, arrived, marks,
    cut, lbuf, ubuf, ustack, inv, istack, blocks,
    chain_send, side_send, half_recv, row_send, row_recv,
    table, label_rows, labels, where, load_sem, misc_sem, send, recv, mid_recv, label_send, label_recv, gate,
):
    row = lax.axis_index("row")
    col = lax.axis_index("col")
    n = nrow * ncol
    me = row * ncol + col
    chips = ncol // 2
    chip = col // 2
    core = col % 2
    paths = chip_paths(chips)
    nk, rows_all, kc = lbuf.shape
    cols_all = acc.shape[1]
    edge = blocks.shape[1]
    half = rows_all // 2
    ts = half // STEPS
    us = kc // STEPS
    shift = width // ts
    mid = nk // 2
    nexts = [pick(chip, list(zip(p[:-1], p[1:])), 0) for p in paths]
    places = [pick(chip, [(c, at) for at, c in enumerate(p)], 0) for p in paths]
    total = nk * STEPS
    fine = total * FINE
    ls = ts // FINE
    us = us // FINE

    def tile_rows(h, tile):
        return pl.ds(pl.multiple_of(h * half + tile * ts, ts), ts)

    def l_copy(h, t, send_sem, target):
        tile = (t // FINE % STEPS + shift) % STEPS
        first = pl.multiple_of(h * half + tile * ts + t % FINE * ls, ls)
        at = lbuf.at[t // FINE // STEPS, pl.ds(first, ls), :]
        return pltpu.make_async_remote_copy(
            src_ref=at, dst_ref=at,
            send_sem=send_sem.at[h, t], recv_sem=half_recv.at[h, t],
            device_id=(row, target), device_id_type=MESH,
        )

    def u_copy(src, t):
        s = pl.ds(pl.multiple_of(t * us, us), us)
        return pltpu.make_async_remote_copy(
            src_ref=src.at[s, :], dst_ref=ubuf.at[s, :],
            send_sem=row_send.at[t], recv_sem=row_recv.at[t],
            device_id=(row + 1, col), device_id_type=MESH,
        )

    def load(h, i):
        s = tile_rows(h, (i + shift) % STEPS)
        return pltpu.make_async_copy(front.at[s, :], acc.at[s, :], load_sem.at[h, i])

    def load_inv(p):
        return pltpu.make_async_copy(inverses.at[p], inv, misc_sem.at[0])

    load_rows = pltpu.make_async_copy(
        front.at[pl.ds(0, width), :], ubuf.at[pl.ds(0, width), :], misc_sem.at[1]
    )
    piece = rows_all // ncol

    def panel_store(k):
        return pltpu.make_async_copy(
            lbuf.at[k, pl.ds(pl.multiple_of(col * piece, piece), piece), :],
            panels.at[:, pl.ds(k * kc, kc)], misc_sem.at[2 + k],
        )

    def active(r, c):
        return r * brows + brows - 1 >= c * bcols

    def part(index):
        return pl.ds(index * cap, cap)

    def straight(source, target):
        return pltpu.make_async_remote_copy(
            src_ref=blocks.at[part(target)], dst_ref=arrived.at[part(source)],
            send_sem=send.at[target], recv_sem=recv.at[source],
            device_id=(target // ncol, target % ncol), device_id_type=MESH,
        )

    def hop(to_row, to_col):
        target = to_row * ncol + to_col
        return pltpu.make_async_remote_copy(
            src_ref=blocks.at[part(target)], dst_ref=blocks.at[part(to_row * ncol + col)],
            send_sem=send.at[target], recv_sem=mid_recv.at[to_row * ncol + col],
            device_id=(row, to_col), device_id_type=MESH,
        )

    def landed(to_row, from_col):
        return pltpu.make_async_remote_copy(
            src_ref=blocks.at[part(0)], dst_ref=blocks.at[part(to_row * ncol + from_col)],
            send_sem=send.at[0], recv_sem=mid_recv.at[to_row * ncol + from_col],
            device_id=(row, from_col), device_id_type=MESH,
        )

    def relay(to_row, from_col):
        return pltpu.make_async_remote_copy(
            src_ref=blocks.at[part(to_row * ncol + from_col)],
            dst_ref=arrived.at[part(row * ncol + from_col)],
            send_sem=send.at[to_row * ncol + from_col],
            recv_sem=recv.at[row * ncol + from_col],
            device_id=(to_row, col), device_id_type=MESH,
        )

    def label_copy(source, target):
        return pltpu.make_async_remote_copy(
            src_ref=labels.at[target], dst_ref=marks.at[source],
            send_sem=label_send.at[target], recv_sem=label_recv.at[source],
            device_id=(target // ncol, target % ncol), device_id_type=MESH,
        )

    own_blocks = pltpu.make_async_copy(
        blocks.at[part(me)], arrived.at[part(me)], misc_sem.at[2 + nk]
    )
    own_labels = pltpu.make_async_copy(labels.at[me], marks.at[me], misc_sem.at[3 + nk])

    def local_loads():
        @pl.when(col == 0)
        def _():
            load_inv(0).start()

        def start_load(i, carry):
            for h in range(2):
                load(h, i).start()
            return carry

        lax.fori_loop(0, STEPS, start_load, 0)

        @pl.when(row == 0)
        def _():
            load_rows.start()

    barrier = pltpu.get_barrier_semaphore()

    def greet(d, carry):
        other = (me + d) % n
        pl.semaphore_signal(
            barrier, 1, device_id=(other // ncol, other % ncol), device_id_type=MESH
        )
        return carry

    def make_tables():
        count = brows * bcols
        owner = packed[...] >> bits
        slot = (packed[...] & ((1 << bits) - 1)).astype(jnp.float32)
        hit = owner == lax.broadcasted_iota(jnp.int32, (n, count), 0)
        before = lax.broadcasted_iota(jnp.int32, (count, count), 0) < (
            lax.broadcasted_iota(jnp.int32, (count, count), 1)
        )
        rank = jnp.dot(
            jnp.where(hit, 1.0, 0.0), jnp.where(before, 1.0, 0.0),
            preferred_element_type=jnp.float32,
        )
        position = lax.broadcasted_iota(jnp.int32, (n, count), 1).astype(jnp.float32)
        lane = lax.broadcasted_iota(jnp.int32, (n, 128), 1)
        spots = jnp.zeros((n, 128), jnp.float32)
        names = jnp.full((n, 128), -1.0, jnp.float32)
        for q in range(cap):
            chosen = hit & (rank == q)
            spot = jnp.sum(jnp.where(chosen, position, 0.0), axis=1, keepdims=True)
            name = jnp.sum(jnp.where(chosen, slot + 1.0, 0.0), axis=1, keepdims=True) - 1.0
            spots = jnp.where(lane == q, spot, spots)
            names = jnp.where(lane == q, name, names)
        table[...] = spots.astype(jnp.int32)
        label_rows[...] = names.astype(jnp.int32)

        def spread_label(d, carry):
            labels[d] = jnp.broadcast_to(label_rows[pl.ds(d, 1), :], labels.shape[1:])
            return carry

        lax.fori_loop(0, n, spread_label, 0)

    lax.fori_loop(1, n, greet, 0)
    local_loads()
    make_tables()
    pl.semaphore_wait(barrier, n - 1)
    load_table = pltpu.make_async_copy(table, where, misc_sem.at[4 + nk])
    load_table.start()

    @pl.when(core == 1)
    def _():
        def early(u, carry):
            for h in range(2):
                t = u - LAG * jnp.maximum(places[h] - 1, 0)

                @pl.when((t >= 0) & (t < fine))
                def _(h=h, t=t):
                    l_copy(h, t, chain_send, 0).wait_recv()
                    if chips > 1:
                        @pl.when(places[h] < chips - 1)
                        def _():
                            l_copy(h, t, chain_send, nexts[h] * 2 + 1).start()

                    @pl.when(chip > 0)
                    def _():
                        l_copy(h, t, side_send, chip * 2).start()

            return carry

        lax.fori_loop(0, fine + LAG * max(chips - 2, 0), early, 0)

    def stacked(value):
        high, low = split3(value, 1)
        return jnp.concatenate([high, high, low], axis=1)

    def split_rows(source, target, depth):
        high, low = split3(source, 0)
        target[pl.ds(0, depth), :] = high
        target[pl.ds(depth, depth), :] = low
        target[pl.ds(2 * depth, depth), :] = high

    def update(k, i):
        @pl.when(i == 0)
        def _():
            for q in range(cols_all // edge // 2):
                s = pl.ds(q * 2 * edge, 2 * edge)
                split_rows(
                    ubuf[pl.ds(pl.multiple_of(k * kc, kc), kc), s], ustack.at[:, s], kc
                )

        t = k * STEPS + i
        tile = (i + shift) % STEPS

        @pl.when((core == 0) & (col > 0))
        def _():
            for h in range(2):
                for g in range(FINE):
                    l_copy(h, t * FINE + g, chain_send, 0).wait_recv()

        both = jnp.concatenate([lbuf[k, tile_rows(h, tile), :] for h in range(2)], axis=0)
        a = stacked(both)
        for q in range(cols_all // edge // 2):
            s = pl.ds(q * 2 * edge, 2 * edge)
            out = jnp.dot(a, ustack[:, s], preferred_element_type=jnp.float32)
            for h in range(2):
                at = tile_rows(h, tile)
                acc[at, s] = acc[at, s] - out[h * ts:(h + 1) * ts]

        @pl.when(k == nk - 1)
        def _():
            for h in range(2):
                for u in range(ts // edge):
                    at = pl.ds(pl.multiple_of(h * half + tile * ts + u * edge, edge), edge)
                    first = ((h * STEPS + tile) * (ts // edge) + u) * bcols
                    for q in range(bcols):
                        cut[first + q] = acc[at, pl.ds(q * edge, edge)]

        @pl.when((row == 0) & (k == mid - 1) & (i < width // ts))
        def _():
            at = tile_rows(0, tile)
            ubuf[at, :] = acc[at, :]

    def produce(k, i):
        p = k // mid

        @pl.when((i == 0) & (k % mid == 0))
        def _():
            load_inv(p).wait()
            for q in range(width // 256):
                s = pl.ds(q * 256, 256)
                split_rows(inv[:, s], istack.at[:, s], width)

            @pl.when(p == 0)
            def _():
                load_inv(1).start()

        tile = (i + shift) % STEPS
        from_col = pl.ds(pl.multiple_of(p * width, width), width)
        both = jnp.concatenate([acc[tile_rows(h, tile), from_col] for h in range(2)], axis=0)
        a = stacked(both)
        spot = pl.ds(pl.multiple_of(k % mid * kc, kc), kc)
        out = jnp.dot(a, istack[:, spot], preferred_element_type=jnp.float32)
        for h in range(2):
            lbuf[k, tile_rows(h, tile), :] = out[h * ts:(h + 1) * ts]

    def step(t, carry):
        k = t // STEPS
        i = t % STEPS

        @pl.when(k == 0)
        def _():
            for h in range(2):
                load(h, i).wait()

        @pl.when((row == 0) & (t == 0))
        def _():
            load_rows.wait()

        @pl.when((col == 0) & (k < nk) & (k % mid != 0))
        def _():
            produce(k, i)

        @pl.when(k > 0)
        def _():
            update(k - 1, i)

        @pl.when((col == 0) & (k < nk) & (k % mid == 0))
        def _():
            produce(k, i)

        @pl.when(k < nk)
        def _():
            @pl.when(col == 0)
            def _():
                for g in range(FINE):
                    for h in range(2):
                        l_copy(h, t * FINE + g, side_send, 1).start()

            if nrow > 1:
                for g in range(FINE):
                    @pl.when(row > 0)
                    def _(g=g):
                        u_copy(ubuf, t * FINE + g).wait_recv()

                    @pl.when(row < nrow - 1)
                    def _(g=g):
                        u_copy(ubuf, t * FINE + g).start()

        if nrow > 1:
            @pl.when((t == total) & (row < nrow - 1) & ((row == 0) | (core == 1)))
            def _():
                def sent(u, carry):
                    u_copy(ubuf, u).wait_send()
                    return carry

                lax.fori_loop(0, fine, sent, 0)
                pl.semaphore_signal(
                    gate, 1, device_id=(row, col + 1 - 2 * core), device_id_type=MESH
                )

        return carry

    if nrow > 1:
        @pl.when((row == 0) & (core == 1))
        def _():
            pl.semaphore_wait(gate, 1)

    lax.fori_loop(0, total + STEPS, step, 0)

    for k in range(nk):
        panel_store(k).start()

    load_table.wait()
    order = [(nrow // 2 + i) % nrow for i in range(nrow)]

    @pl.when(active(row, col))
    def _():
        def take(to_row, to_col):
            target = to_row * ncol + to_col
            for q in range(cap):
                spot = jnp.clip(where[target, q], 0, cut.shape[0] - 1)
                blocks[target * cap + q] = cut[spot]

        def give(to_row, to_col):
            target = to_row * ncol + to_col
            direct = active(row, to_col) | (to_row == row)

            @pl.when((target != me) & direct)
            def _():
                straight(me, target).start()

            @pl.when(jnp.logical_not(direct))
            def _():
                hop(to_row, to_col).start()

        def pieces(lift):
            def both(j, carry):
                to_col = (col + j) % ncol
                for o in order:
                    to_row = (row + o) % nrow

                    @pl.when((to_row > row) == lift)
                    def _(to_row=to_row):
                        give(to_row, to_col)

                return carry

            lax.fori_loop(0, ncol, both, 0)

        def fill(j, carry):
            to_col = (col + j) % ncol
            for o in order:
                take((row + o) % nrow, to_col)

                @pl.when(j > 0)
                def _(o=o):
                    to_row = (row + o) % nrow

                    @pl.when(to_row <= row)
                    def _():
                        give(to_row, (to_col + ncol - 1) % ncol)

            return carry

        lax.fori_loop(0, ncol, fill, 0)
        for o in order:
            @pl.when((row + o) % nrow <= row)
            def _(o=o):
                give((row + o) % nrow, (col + ncol - 1) % ncol)

        if nrow > 1:
            @pl.when((core == 0) & (row < nrow - 1))
            def _():
                pl.semaphore_wait(gate, 1)

        pieces(True)

        def label_step(d, carry):
            label_copy(me, (me + d) % n).start()
            return carry

        lax.fori_loop(1, n, label_step, 0)
        own_blocks.start()
        own_labels.start()

    def pass_on(act, lift):
        def body(j, carry):
            from_col = 2 * j % ncol + 2 * j // ncol

            @pl.when(active(row, from_col))
            def _():
                for o in order:
                    to_row = (row + o) % nrow

                    @pl.when((to_row != row) & ((to_row > row) == lift))
                    def _(to_row=to_row):
                        act(to_row, from_col)

            return carry

        @pl.when(jnp.logical_not(active(row, col)))
        def _():
            lax.fori_loop(0, ncol, body, 0)

    def forward(to_row, from_col):
        landed(to_row, from_col).wait_recv()
        relay(to_row, from_col).start()

    pass_on(forward, False)
    if nrow > 1:
        @pl.when((core == 0) & (row < nrow - 1) & jnp.logical_not(active(row, col)))
        def _():
            pl.semaphore_wait(gate, 1)

    pass_on(forward, True)

    def drain_l(t, carry):
        for h in range(2):
            @pl.when((col == 0) | ((core == 1) & (chip > 0)))
            def _(h=h):
                l_copy(h, t, side_send, 0).wait_send()

            if chips > 1:
                @pl.when((core == 1) & (places[h] < chips - 1))
                def _(h=h):
                    l_copy(h, t, chain_send, 0).wait_send()

        if nrow > 1:
            @pl.when((row < nrow - 1) & (row > 0) & (core == 0))
            def _():
                u_copy(ubuf, t).wait_send()

        return carry

    lax.fori_loop(0, fine, drain_l, 0)

    for k in range(nk):
        panel_store(k).wait()

    def arrive(s, carry):
        @pl.when((s != me) & active(s // ncol, s % ncol))
        def _():
            label_copy(s, 0).wait_recv()
            straight(s, 0).wait_recv()

        return carry

    lax.fori_loop(0, n, arrive, 0)

    @pl.when(active(row, col))
    def _():
        def drain(d, carry):
            target = (me + d) % n
            label_copy(me, target).wait_send()
            straight(me, target).wait_send()
            return carry

        lax.fori_loop(1, n, drain, 0)
        own_blocks.wait()
        own_labels.wait()

    for lift in (False, True):
        pass_on(lambda to_row, from_col: relay(to_row, from_col).wait_send(), lift)


def front_update(packed, front, inverses, brows, bcols, bits, cap, edge):
    nrow, ncol = lax.axis_size("row"), lax.axis_size("col")
    n = nrow * ncol
    width = inverses.shape[1]
    rows_all, cols_all = front.shape
    kc = width // 2
    nk = 4
    dma = pltpu.SemaphoreType.DMA
    f32, bf16 = jnp.float32, jnp.bfloat16
    shape = jax.ShapeDtypeStruct
    return pl.pallas_call(
        functools.partial(front_kernel, nrow, ncol, width, cap, brows, bcols, bits),
        out_shape=(
            shape(front.shape, f32),
            shape((rows_all // ncol, 2 * width), f32),
            shape((n * cap, edge, edge), f32),
            shape((n, 8, 128), jnp.int32),
        ),
        in_specs=[VMEM, ANY, ANY],
        out_specs=(VMEM, ANY, ANY, VMEM),
        scratch_shapes=[
            pltpu.VMEM((brows * bcols, edge, edge), f32),
            pltpu.VMEM((nk, rows_all, kc), f32),
            pltpu.VMEM((2 * width, cols_all), f32),
            pltpu.VMEM((3 * kc, cols_all), bf16),
            pltpu.VMEM((width, width), f32),
            pltpu.VMEM((3 * width, width), bf16),
            pltpu.VMEM((n * cap, edge, edge), f32),
            dma((2, nk * STEPS * FINE)), dma((2, nk * STEPS * FINE)),
            dma((2, nk * STEPS * FINE)),
            dma((nk * STEPS * FINE,)), dma((nk * STEPS * FINE,)),
            pltpu.VMEM((n, 128), jnp.int32),
            pltpu.VMEM((n, 128), jnp.int32),
            pltpu.VMEM((n, 8, 128), jnp.int32),
            pltpu.SMEM((n, 128), jnp.int32),
            dma((2, STEPS)), dma((5 + nk,)),
            dma((n,)), dma((n,)), dma((n,)), dma((n,)), dma((n,)),
            pltpu.SemaphoreType.REGULAR,
        ],
        compiler_params=pltpu.CompilerParams(
            has_side_effects=True, collective_id=0, vmem_limit_bytes=(34 << 20) + (n - 32) * (16 << 10)
        ),
        name="front_update",
    )(packed, front, inverses)


def add_kernel(
    ncol, brows, bcols, cap, names, parent, arrived, updated, panels,
    out, updated_out, panels_out, marks, parent_sem, name_sem, out_sem,
):
    n = arrived.shape[0] // cap
    parts = out_sem.shape[0] - 1
    rows = updated.shape[0] // parts

    def each(first, count, body):
        def step(s, carry):
            @pl.when(s // ncol * brows + brows - 1 >= s % ncol * bcols)
            def _():
                body(s)

            return carry

        lax.fori_loop(first, first + count, step, 0)

    def put(i):
        s = pl.ds(i * rows, rows)
        return pltpu.make_async_copy(updated.at[s, :], updated_out.at[s, :], out_sem.at[i])

    put_strip = pltpu.make_async_copy(panels, panels_out, out_sem.at[parts])
    whole = pltpu.make_async_copy(parent, out, parent_sem)
    load_names = pltpu.make_async_copy(names, marks, name_sem)
    load_names.start()
    whole.start()
    for i in range(parts):
        put(i).start()
    put_strip.start()
    load_names.wait()
    whole.wait()

    def add(s):
        for k in range(cap):
            m = marks[s, 0, k]

            @pl.when(m >= 0)
            def _(k=k, m=m):
                out[m] = out[m] + arrived[s * cap + k]

    each(0, n, add)
    for i in range(parts):
        put(i).wait()
    put_strip.wait()


def add_blocks(marks, parent, arrived, updated, panels, brows, bcols, cap):
    n = arrived.shape[0] // cap
    parts = 8
    like = lambda x: jax.ShapeDtypeStruct(x.shape, x.dtype)
    return pl.pallas_call(
        functools.partial(add_kernel, lax.axis_size("col"), brows, bcols, cap),
        out_shape=(like(parent), like(updated), like(panels)),
        in_specs=[ANY, VMEM, VMEM, VMEM, VMEM],
        out_specs=(VMEM, HBM, HBM),
        scratch_shapes=[
            pltpu.SMEM(marks.shape, marks.dtype),
            pltpu.SemaphoreType.DMA,
            pltpu.SemaphoreType.DMA,
            pltpu.SemaphoreType.DMA((parts + 1,)),
        ],
        compiler_params=pltpu.CompilerParams(vmem_limit_bytes=24<<20),
        name="add_blocks",
    )(marks, parent, arrived, updated, panels)


def local(front, inverses, block_owner, block_slot, parent_in):
    devices = lax.axis_size("row") * lax.axis_size("col")
    brows, bcols = block_owner.shape
    edge = parent_in.shape[1]
    count = brows * bcols
    cap = max(1, (count + devices - 1) // devices)
    bits = max(1, (parent_in.shape[0] - 1).bit_length())
    packed = ((block_owner << bits) + block_slot).reshape(1, count)
    updated, panels, arrived, marks = front_update(
        packed, front, inverses, brows, bcols, bits, cap, edge
    )
    parent_out, updated, panels = add_blocks(
        marks, parent_in, arrived, updated, panels, brows, bcols, cap
    )
    return (updated, panels, parent_out)


def solution(mesh):
    in_specs = (
        P("row", "col"),
        P(),
        P("row", "col"),
        P("row", "col"),
        P(("row", "col"), None, None),
    )
    out_specs = (P("row", "col"), P(("row", "col"), None), P(("row", "col"), None, None))
    return jax.shard_map(local, mesh=mesh, in_specs=in_specs, out_specs=out_specs, check_vma=False)
```
